32 devices in a mesh: groups: 2 (over x), mp: 4 (over y, core), dp: 4 (over z).
Axes of the slice: x: 2, y: 2, z: 4, core: 2. Of those that a mesh axis runs over, the one named last changes fastest.
Arguments:
- grid_feat: bfloat16 [8, 512, 1024], P(('groups', 'dp'), 'mp'), parts along dimension 0, may hold values from -6 to 6
- node_feat: bfloat16 [8, 256, 1024], P(('groups', 'dp'), 'mp'), parts along dimension 0, may hold values from -6 to 6
- cotangent: bfloat16 [8, 512, 1024], P(('groups', 'dp'), 'mp'), parts along dimension 0, may hold values from -6 to 6
- w_query: bfloat16 [1024, 1024], replicated, may hold values from -2 to 2, as said below
- w_keyval: bfloat16 [1024, 2048], replicated, may hold values from -2 to 2, as said below
- neighbours: int32 [512, 12], P('mp'), may hold values from 0 to 127, as said below
- send_rows: int32 [4, 4, 16], P('mp'), may hold values from 0 to 63, as said below
Outputs:
- d_grid: bfloat16 [8, 512, 1024], P(('groups', 'dp'), 'mp'), parts along dimension 0
- d_nodes: bfloat16 [8, 256, 1024], P(('groups', 'dp'), 'mp'), parts along dimension 0
- dw_query: float32 [2048, 1024], P(('groups', 'mp', 'dp')), parts along dimension 0
- dw_keyval: float32 [2048, 2048], P(('groups', 'mp', 'dp')), parts along dimension 0
The draws below stay inside these ranges and needn't reach their ends.
There are 2 independent parts, one for each index of `groups`. The reference program is written for one: setup_inputs(seed, part) draws one part's arguments, and reference() takes and returns one part's arrays. A program takes and returns all parts, laid end to end along the dimension named above; an argument that names none is the same for every part. Nothing has to cross between parts.
Inputs may be any that keep to these rules, and one draw needn't show every extreme that they name: `neighbours`: an entry under 4 * 16 names slot r % 16 of the block that index r // 16 of mp sends to the grid point's own index; larger entries name the own index's nodes. The slots that are named in a block form a leading run; every index names all 16 slots of the blocks from the indices one below and one above it on mp (wrapping around), some of every other index's block, and none of its own block. `send_rows`: the 16 rows of one block are distinct local node rows of the sending index. `w_query`: projection weights. `w_keyval`: projection weights.
All inputs are finite; a program needn't handle non-finite values.
Results may differ from the reference program's by a relative error of at most 0.018.
The reference program's roundings to bfloat16 on the way count: a program that leaves them out, or rounds other values in their place, can miss the bound.
Values may be sent and summed in bfloat16 or wider, within the bound.
A program may use at most 128 MiB of HBM per device.

```python
import jax
import jax.numpy as jnp
from jax import lax

D = 1024
HEADS = 16
NBR = 12
GRID_DEV = 128
NODE_DEV = 64
CAP = 16
SAMPLES = 4
GRID = 512
NODES = 256
N_MP = 4


def plan_counts(key):
    sender = jnp.arange(N_MP)[:, None]
    target = jnp.arange(N_MP)[None, :]
    counts = jax.random.randint(jax.random.fold_in(key, 7), (N_MP, N_MP), max(1, CAP // 4), CAP + 1)
    beside = ((target - sender) % N_MP == 1) | ((sender - target) % N_MP == 1)
    counts = jnp.where(beside, CAP, counts)
    return jnp.where(sender == target, 0, counts).astype(jnp.int32)


def draw_neighbours(key, part):
    counts = plan_counts(key)
    ends = jnp.cumsum(counts, axis=0)
    starts = ends - counts
    total = ends[-1]
    device = jnp.arange(GRID) // GRID_DEV
    total_rows = total[device][:, None]
    pick = jax.random.randint(jax.random.fold_in(key, 11), (GRID, NBR), 0, NODE_DEV + total_rows)
    ends_rows = ends[:, device].T
    source = jnp.sum(ends_rows[:, None, :] <= pick[:, :, None], axis=2)
    source_cl = jnp.minimum(source, N_MP - 1)
    begin = starts[source_cl, device[:, None]]
    remote = source_cl * CAP + (pick - begin)
    local = N_MP * CAP + (pick - total_rows)
    value = jnp.where(pick < total_rows, remote, local)
    first = jnp.arange(GRID) % GRID_DEV
    column = jnp.where(first == 0, N_MP * CAP + NODE_DEV - 1, jnp.where((first == 1) & (device > 0), 0, value[:, 0]))
    value = value.at[:, 0].set(column)
    return value.astype(jnp.int32)


def pin_value(perm, slot, target):
    current = perm[slot]
    perm = jnp.where(perm == target, current, perm)
    return perm.at[slot].set(target)


def draw_send_rows(key, part):
    base = jax.random.fold_in(key, 23)

    def one_block(index):
        perm = jax.random.permutation(jax.random.fold_in(base, index), NODE_DEV)
        pinned = pin_value(pin_value(perm, 0, NODE_DEV - 1), 1, 0)
        return jnp.where(index == 1, pinned, perm)[:CAP]
    rows = jax.vmap(one_block)(jnp.arange(N_MP * N_MP))
    return rows.reshape(N_MP, N_MP, CAP).astype(jnp.int32)


def draw_w_query(key, part):
    base = jnp.clip(jax.random.normal(jax.random.fold_in(key, 31), (D, D), jnp.float32), -4.0, 4.0) * D ** (-0.5)
    return base.astype(jnp.bfloat16)


def draw_w_keyval(key, part):
    base = jnp.clip(jax.random.normal(jax.random.fold_in(key, 37), (D, 2 * D), jnp.float32), -4.0, 4.0) * D ** (-0.5)
    return base.astype(jnp.bfloat16)


def strengthened(values, own_key, source, target, shards_of, factor):
    def block_of(dim):
        return (jnp.arange(values.shape[dim]) // (values.shape[dim] // shards_of)).reshape((-1,) + (1,) * (values.ndim - 1 - dim))

    near = jax.random.permutation(own_key, shards_of)[block_of(target)]
    far = (block_of(target) + shards_of // 2) % shards_of
    return jnp.where((block_of(source) == near) | (block_of(source) == far), factor * values, values)


def block_levels(key, extent, shards, low, high):
    def one(position, blocks):
        heights = jax.random.uniform(jax.random.fold_in(jax.random.fold_in(key, 6), position), (blocks,), jnp.float32, low / len(shards), high / len(shards))
        return jnp.repeat(jnp.exp(heights), extent[position] // blocks).reshape((-1,) + (1,) * (len(extent) - position - 1))

    loudness = one(*shards[0])
    for cut in shards[1:]:
        loudness = loudness * one(*cut)
    return loudness


def bell_draw(own_key, shape, scale, bound, shards=(), held_as=jnp.bfloat16):
    array = jax.random.normal(own_key, shape, jnp.float32) * scale
    if len(shards) > 0:
        array = block_levels(own_key, shape, shards, -0.22, 0.18) * array
    return jnp.clip(array, min=-bound, max=bound).astype(held_as)


def noise_with(rng, extent, scale, limit, shards, heavy, held_as=jnp.bfloat16):
    entries = scale * jax.random.normal(rng, extent, jnp.float32)
    if shards:
        entries = entries * block_levels(rng, extent, shards, -0.22, 0.18)
    return jnp.clip(strengthened(entries, jax.random.fold_in(rng, 3), *heavy), -limit, limit).astype(held_as)


def setup_inputs(seed: int = 0, part: int = 0) -> dict:
    seeds = jax.random.split(jax.random.key(seed), 8)
    part_keys = jax.random.split(jax.random.fold_in(seeds[7], part), 8)
    return {
        "grid_feat": noise_with(part_keys[0], (SAMPLES, GRID, D), 1.0, 6.0, ((0, 4), (1, 4)), (1, 2, 4, 2.0)),
        "node_feat": noise_with(part_keys[1], (SAMPLES, NODES, D), 1.0, 6.0, ((0, 4), (1, 4)), (1, 2, 4, 2.0)),
        "cotangent": bell_draw(part_keys[2], (SAMPLES, GRID, D), 1.0, 6.0, ((0, 4), (1, 4))),
        "w_query": draw_w_query(jax.random.fold_in(seeds[7], 71), part),
        "w_keyval": draw_w_keyval(jax.random.fold_in(seeds[7], 71), part),
        "neighbours": draw_neighbours(jax.random.fold_in(seeds[7], 71), part),
        "send_rows": draw_send_rows(jax.random.fold_in(seeds[7], 71), part),
    }


def edge_grads(query_rows, cot_rows, edges):
    count = query_rows.shape[0]
    width = query_rows.shape[1]
    nbrs = edges.shape[1]
    scale = (width // HEADS) ** -0.5
    query = query_rows.astype(jnp.float32).reshape(count, HEADS, -1)
    cot = cot_rows.astype(jnp.float32).reshape(count, HEADS, -1)
    keys = edges[:, :, :width].astype(jnp.float32).reshape(count, nbrs, HEADS, -1)
    values = edges[:, :, width:].astype(jnp.float32).reshape(count, nbrs, HEADS, -1)
    scores = jnp.einsum('ghe,gkhe->gkh', query, keys) * scale
    attn = jax.nn.softmax(scores, axis=1)
    d_attn = jnp.einsum('ghe,gkhe->gkh', cot, values)
    d_scores = attn * (d_attn - jnp.sum(attn * d_attn, axis=1, keepdims=True))
    d_query = (jnp.einsum('gkh,gkhe->ghe', d_scores, keys) * scale).reshape(count, width).astype(jnp.bfloat16)
    d_keys = d_scores[..., None] * query[:, None] * scale
    d_values = attn[..., None] * cot[:, None]
    contrib = jnp.concatenate([d_keys.reshape(count, nbrs, width), d_values.reshape(count, nbrs, width)], axis=-1)
    return d_query, contrib


def reference(grid_feat, node_feat, cotangent, w_query, w_keyval, neighbours, send_rows):
    shard = (jnp.arange(GRID) // GRID_DEV).astype(jnp.int32)
    remote = neighbours < N_MP * CAP
    source = jnp.minimum(neighbours // CAP, N_MP - 1).astype(jnp.int32)
    slot = (neighbours % CAP).astype(jnp.int32)
    remote_node = source * NODE_DEV + send_rows[source, shard[:, None], slot]
    local_node = shard[:, None] * NODE_DEV + neighbours - N_MP * CAP
    node_id = jnp.where(remote, remote_node, local_node).astype(jnp.int32)
    wscale = 1.0 / (SAMPLES * GRID) ** 0.5
    dims_t = (((0,), (0,)), ((), ()))

    def one_sample(carry, inputs):
        grid_x, node_x, cot = inputs
        query = jnp.dot(grid_x, w_query, preferred_element_type=jnp.float32).astype(jnp.bfloat16)
        keyval = jnp.dot(node_x, w_keyval, preferred_element_type=jnp.float32).astype(jnp.bfloat16)

        def shard_step(acc, index):
            start = (index * GRID_DEV).astype(jnp.int32)
            query_rows = lax.dynamic_slice_in_dim(query, start, GRID_DEV, 0)
            cot_rows = lax.dynamic_slice_in_dim(cot, start, GRID_DEV, 0)
            ids = lax.dynamic_slice_in_dim(node_id, start, GRID_DEV, 0)
            d_query, contrib = edge_grads(query_rows, cot_rows, keyval[ids])
            partial_value = jax.ops.segment_sum(contrib.reshape(-1, 2 * D), ids.reshape(-1), num_segments=NODES)
            partial_value = lax.optimization_barrier(partial_value.astype(jnp.bfloat16))
            return acc + partial_value.astype(jnp.float32), d_query

        dkv_sum, d_query = lax.scan(shard_step, jnp.zeros((NODES, 2 * D), jnp.float32), jnp.arange(N_MP, dtype=jnp.int32))
        d_query = d_query.reshape(GRID, D)
        dkv = dkv_sum.astype(jnp.bfloat16)
        d_grid = jnp.dot(d_query, w_query.T, preferred_element_type=jnp.float32).astype(jnp.bfloat16)
        d_nodes = jnp.dot(dkv, w_keyval.T, preferred_element_type=jnp.float32).astype(jnp.bfloat16)
        grad_q = carry[0] + lax.dot_general(grid_x, d_query, dims_t, preferred_element_type=jnp.float32) * wscale
        grad_kv = carry[1] + lax.dot_general(node_x, dkv, dims_t, preferred_element_type=jnp.float32) * wscale
        return (grad_q, grad_kv), (d_grid, d_nodes)

    start = (jnp.zeros((D, D), jnp.float32), jnp.zeros((D, 2 * D), jnp.float32))
    (grad_q, grad_kv), (d_grid, d_nodes) = lax.scan(one_sample, start, (grid_feat, node_feat, cotangent))
    return d_grid, d_nodes, grad_q, grad_kv
```

```python
import functools
import math

import jax
import jax.numpy as jnp
from jax import lax
from jax.experimental import pallas as pl
from jax.experimental.pallas import tpu as pltpu
from jax.sharding import PartitionSpec as P

HEADS = 16
LANES = 128
MESH = pl.DeviceIdType.MESH
F32 = jnp.float32
BF16 = jnp.bfloat16


def dot_nn(x, y):
    return lax.dot_general(x, y, (((1,), (0,)), ((), ())), preferred_element_type=F32)


def dot_nt(x, y):
    return lax.dot_general(x, y, (((1,), (1,)), ((), ())), preferred_element_type=F32)


def dot_tn(x, y):
    return lax.dot_general(x, y, (((0,), (0,)), ((), ())), preferred_element_type=F32)


def kernel(
    n, nd, wscale,
    gf, nf, cot, wq_h, wkv_h, nbr, sr_col, sr_row,
    dgrid, dnodes, dwq, dwkv,
    wq, wkv, out_feat, tab, q_s, kv_s, count_s, gf_all, nf_all, dq_s, dq_all,
    part_s, ret_s, dkv_s, dkv_all, tq, tkv, rq, rkv, oq, okv, swq, swkv,
    local_sem, feat_ss, feat_rs, half_ss, half_rs, dq_ss, dq_rs, ret_ss, ret_rs,
    dkv_ss, dkv_rs, z_ss, z_rs, sw_ss, sw_rs,
):
    grid_dev, width = gf.shape
    nodes = nf.shape[0]
    slots = sr_col.shape[0]
    rows = slots + nodes
    cap = slots // n
    nbrs = nbr.shape[1]
    a = width // gf_all.shape[2]
    b = n // a
    high = width // a
    wide = width // b
    out_rows = dwq.shape[0]
    head = width // HEADS
    per = LANES // head
    scale = head ** (-0.5)
    me = lax.axis_index("mp")
    zd = lax.axis_index("dp")
    mine_i = me // b
    mine_j = lax.rem(me, b)

    def to_mp(src, dst, ssem, rsem, peer):
        return pltpu.make_async_remote_copy(
            src_ref=src, dst_ref=dst, send_sem=ssem, recv_sem=rsem,
            device_id={"mp": peer}, device_id_type=MESH,
        )

    def to_dp(src, dst, ssem, rsem, peer):
        return pltpu.make_async_remote_copy(
            src_ref=src, dst_ref=dst, send_sem=ssem, recv_sem=rsem,
            device_id={"dp": peer}, device_id_type=MESH,
        )

    def peer_of(o):
        return lax.rem(me + o, n)

    load_q = pltpu.make_async_copy(wq_h, wq, local_sem.at[0])
    load_kv = pltpu.make_async_copy(wkv_h, wkv, local_sem.at[1])
    load_q.start()
    load_kv.start()
    barrier = pltpu.get_barrier_semaphore()
    for o in range(1, n):
        pl.semaphore_signal(barrier, inc=1, device_id={"mp": peer_of(o)}, device_id_type=MESH)
    for o in range(1, nd):
        pl.semaphore_signal(
            barrier, inc=1, device_id={"dp": lax.rem(zd + o, nd)}, device_id_type=MESH
        )
    pick = (sr_col[...] == lax.broadcasted_iota(jnp.int32, (slots, nodes), 1)).astype(BF16)
    out_feat[...] = dot_nn(pick, nf[...]).astype(BF16)
    tab[pl.ds(slots, nodes), :] = nf[...]
    own_slots = pl.ds(pl.multiple_of(me * cap, cap), cap)
    tab[own_slots, :] = jnp.zeros((cap, width), BF16)
    for jb in range(b):
        ret_s[jb, own_slots, :] = jnp.zeros((cap, 2 * wide), BF16)
    pl.semaphore_wait(barrier, n - 1 + nd - 1)

    feat = []
    for o in range(1, n):
        there = pl.ds(pl.multiple_of(peer_of(o) * cap, cap), cap)
        feat.append(
            to_mp(out_feat.at[there], tab.at[own_slots], feat_ss.at[o], feat_rs.at[o], peer_of(o))
        )
        feat[-1].start()

    ids = nbr[...]
    row_id = lax.broadcasted_iota(jnp.int32, (grid_dev, rows), 1)
    count = jnp.zeros((grid_dev, rows), F32)
    for k in range(nbrs):
        count += (ids[:, k : k + 1] == row_id).astype(F32)
    for s in range(per):
        count_s[s * grid_dev : (s + 1) * grid_dev, :] = count
    half_cols = pl.ds(pl.multiple_of(mine_i * high, high), high)
    gf_all[me] = gf[:, half_cols]
    nf_all[me] = nf[:, half_cols]
    load_q.wait()
    q_s[...] = dot_nn(gf[...], wq[...]).astype(BF16)
    for c in feat:
        c.wait_recv()
    half = []
    for o in range(1, n):
        there = pl.ds(pl.multiple_of((peer_of(o) // b) * high, high), high)
        half.append(
            to_mp(nf.at[:, there], nf_all.at[me], half_ss.at[0, o], half_rs.at[0, o], peer_of(o))
        )
        half.append(
            to_mp(gf.at[:, there], gf_all.at[me], half_ss.at[1, o], half_rs.at[1, o], peer_of(o))
        )
    for c in half:
        c.start()
    load_kv.wait()
    kv_s[...] = dot_nn(tab[...], wkv[...]).astype(BF16)

    lane = lax.broadcasted_iota(jnp.int32, (1, LANES), 1)
    keep = [(lane // head) == s for s in range(per)]

    def spread(x):
        return jnp.concatenate([jnp.where(m, x, jnp.zeros_like(x)) for m in keep], axis=0)

    dq_copies = []
    ret_copies = []
    for jb in range(b):

        def one(blk, carry):
            off = pl.multiple_of(jb * wide + blk * LANES, LANES)
            at = pl.ds(off, LANES)
            at_v = pl.ds(pl.multiple_of(width + off, LANES), LANES)
            here = pl.ds(pl.multiple_of(blk * LANES, LANES), LANES)
            here_v = pl.ds(pl.multiple_of(wide + blk * LANES, LANES), LANES)
            qs = spread(q_s[:, at])
            cs = spread(cot[:, at])
            keys = kv_s[:, at]
            values = kv_s[:, at_v]
            times = count_s[...]
            scores = dot_nt(qs, keys) * scale
            d_attn = dot_nt(cs, values)
            top = jnp.max(
                jnp.where(times > 0, scores, -jnp.inf), axis=1, keepdims=True
            )
            e = jnp.where(times > 0, times * jnp.exp(jnp.minimum(scores - top, 0.0)), 0.0)
            attn = e / jnp.sum(e, axis=1, keepdims=True)
            ds = attn * (d_attn - jnp.sum(attn * d_attn, axis=1, keepdims=True)) * scale
            ds = ds.astype(BF16)
            attn = attn.astype(BF16)
            dq = None
            for s in range(per):
                term = dot_nn(
                    ds[s * grid_dev : (s + 1) * grid_dev],
                    jnp.where(keep[s], keys, jnp.zeros_like(keys)),
                )
                dq = term if dq is None else dq + term
            dq_s[jb, :, here] = dq.astype(BF16)
            part_s[jb, :, here] = dot_tn(ds, qs).astype(BF16)
            part_s[jb, :, here_v] = dot_tn(attn, cs).astype(BF16)
            return carry

        lax.fori_loop(0, wide // LANES, one, 0)
        for o in range(1, n):
            peer = peer_of(o)
            c = to_mp(dq_s.at[jb], dq_all.at[me], dq_ss.at[o], dq_rs.at[o], peer)

            @pl.when(lax.rem(peer, b) == jb)
            def _():
                c.start()

        for o in range(1, n):
            there = pl.ds(pl.multiple_of(peer_of(o) * cap, cap), cap)
            c = to_mp(
                part_s.at[jb, there], ret_s.at[jb, own_slots],
                ret_ss.at[jb, o], ret_rs.at[jb, o], peer_of(o),
            )
            c.start()
            ret_copies.append(c)

    dq_all[me] = dq_s[mine_j]
    acc = None
    for jb in range(b):
        term = dot_nt(dq_s[jb], wq[:, jb * wide : (jb + 1) * wide])
        acc = term if acc is None else acc + term
    dgrid[...] = acc.astype(BF16)

    place = (sr_row[...] == lax.broadcasted_iota(jnp.int32, (nodes, slots), 0)).astype(BF16)
    for jb in range(b):
        for o in range(1, n):
            ret_copies[jb * (n - 1) + o - 1].wait_recv()
        dkv = part_s[jb, slots:, :].astype(F32) + dot_nn(place, ret_s[jb])
        dkv_s[jb] = dkv.astype(BF16)
        for o in range(1, n):
            peer = peer_of(o)
            c = to_mp(dkv_s.at[jb], dkv_all.at[me], dkv_ss.at[o], dkv_rs.at[o], peer)

            @pl.when(lax.rem(peer, b) == jb)
            def _():
                c.start()

    dkv_all[me] = dkv_s[mine_j]

    def got(src, dst, ssem, rsem):
        return to_mp(src, dst, ssem, rsem, peer_of(1))

    for c in half:
        c.wait_recv()
    for o in range(1, n):
        got(dq_s.at[0], dq_all.at[me], dq_ss.at[o], dq_rs.at[o]).wait_recv()
    term_q = dot_tn(
        gf_all[...].reshape(n * grid_dev, high), dq_all[...].reshape(n * grid_dev, wide)
    ) * wscale
    term_q = term_q.astype(BF16).reshape(b, nd, out_rows, wide)
    for d in range(nd):
        tq[d] = term_q[:, d]
    z_copies = []
    for o in range(1, nd):
        peer = lax.rem(zd + o, nd)
        z_copies.append(to_dp(tq.at[peer], rq.at[o], z_ss.at[0, o], z_rs.at[0, o], peer))
        z_copies[-1].start()

    acc = None
    for jb in range(b):
        for k in range(2):
            term = dot_nt(
                dkv_s[jb, :, k * wide : (k + 1) * wide],
                wkv[:, k * width + jb * wide : k * width + (jb + 1) * wide],
            )
            acc = term if acc is None else acc + term
    dnodes[...] = acc.astype(BF16)

    for o in range(1, n):
        got(dkv_s.at[0], dkv_all.at[me], dkv_ss.at[o], dkv_rs.at[o]).wait_recv()
    term_kv = dot_tn(
        nf_all[...].reshape(n * nodes, high), dkv_all[...].reshape(n * nodes, 2 * wide)
    ) * wscale
    term_kv = term_kv.astype(BF16).reshape(b, nd, out_rows, 2 * wide)
    for d in range(nd):
        tkv[d] = term_kv[:, d]
    for o in range(1, nd):
        peer = lax.rem(zd + o, nd)
        z_copies.append(to_dp(tkv.at[peer], rkv.at[o], z_ss.at[1, o], z_rs.at[1, o], peer))
        z_copies[-1].start()

    def finish(which, t, r, out, sw, width_out):
        total = t[zd].astype(F32)
        for o in range(1, nd):
            z_copies[which * (nd - 1) + o - 1].wait_recv()
            total += r[o].astype(F32)
        out[...] = total.astype(BF16)
        sent = []
        for o in range(1, b):
            mate = lax.rem(mine_j + o, b)
            c = to_mp(
                out.at[mate], sw.at[o], sw_ss.at[which, o], sw_rs.at[which, o],
                mine_i * b + mate,
            )
            c.start()
            sent.append(c)
        return sent

    sent_q = finish(0, tq, rq, oq, swq, wide)
    sent_kv = finish(1, tkv, rkv, okv, swkv, 2 * wide)

    def columns(j, k):
        return pl.ds(pl.multiple_of(k * width + j * wide, LANES), wide)

    dwq[:, columns(mine_j, 0)] = oq[mine_j].astype(F32)
    for o in range(1, b):
        source = lax.rem(mine_j + b - o, b)
        sent_q[o - 1].wait_recv()
        dwq[:, columns(source, 0)] = swq[o].astype(F32)
    for k in range(2):
        dwkv[:, columns(mine_j, k)] = okv[mine_j][:, k * wide : (k + 1) * wide].astype(F32)
    for o in range(1, b):
        source = lax.rem(mine_j + b - o, b)
        sent_kv[o - 1].wait_recv()
        for k in range(2):
            dwkv[:, columns(source, k)] = swkv[o][:, k * wide : (k + 1) * wide].astype(F32)

    for c in feat + half + ret_copies + z_copies + sent_q + sent_kv:
        c.wait_send()
    for o in range(1, n):
        got(dq_s.at[0], dq_all.at[me], dq_ss.at[o], dq_rs.at[o]).wait_send()
        got(dkv_s.at[0], dkv_all.at[me], dkv_ss.at[o], dkv_rs.at[o]).wait_send()


def per_device(grid_feat, node_feat, cotangent, w_query, w_keyval, neighbours, send_rows):
    n = lax.axis_size("mp")
    nd = lax.axis_size("dp")
    samples_dev, grid_dev, width = grid_feat.shape
    nodes = node_feat.shape[1]
    cap = send_rows.shape[2]
    slots = n * cap
    rows = slots + nodes
    a = 2
    b = n // a
    high = width // a
    wide = width // b
    out_rows = width // (n * nd)
    per = LANES * HEADS // width
    wscale = 1.0 / math.sqrt(samples_dev * nd * grid_dev * n)
    vmem = pl.BlockSpec(memory_space=pltpu.VMEM)
    anywhere = pl.BlockSpec(memory_space=pl.ANY)
    dma = pltpu.SemaphoreType.DMA
    d_grid, d_nodes, dw_query, dw_keyval = pl.pallas_call(
        functools.partial(kernel, n, nd, wscale),
        out_shape=(
            jax.ShapeDtypeStruct((grid_dev, width), BF16),
            jax.ShapeDtypeStruct((nodes, width), BF16),
            jax.ShapeDtypeStruct((out_rows, width), F32),
            jax.ShapeDtypeStruct((out_rows, 2 * width), F32),
        ),
        in_specs=[vmem, vmem, vmem, anywhere, anywhere, vmem, vmem, vmem],
        out_specs=(vmem, vmem, vmem, vmem),
        scratch_shapes=[
            pltpu.VMEM((width, width), BF16),
            pltpu.VMEM((width, 2 * width), BF16),
            pltpu.VMEM((slots, width), BF16),
            pltpu.VMEM((rows, width), BF16),
            pltpu.VMEM((grid_dev, width), BF16),
            pltpu.VMEM((rows, 2 * width), BF16),
            pltpu.VMEM((per * grid_dev, rows), F32),
            pltpu.VMEM((n, grid_dev, high), BF16),
            pltpu.VMEM((n, nodes, high), BF16),
            pltpu.VMEM((b, grid_dev, wide), BF16),
            pltpu.VMEM((n, grid_dev, wide), BF16),
            pltpu.VMEM((b, rows, 2 * wide), BF16),
            pltpu.VMEM((b, slots, 2 * wide), BF16),
            pltpu.VMEM((b, nodes, 2 * wide), BF16),
            pltpu.VMEM((n, nodes, 2 * wide), BF16),
            pltpu.VMEM((nd, b, out_rows, wide), BF16),
            pltpu.VMEM((nd, b, out_rows, 2 * wide), BF16),
            pltpu.VMEM((nd, b, out_rows, wide), BF16),
            pltpu.VMEM((nd, b, out_rows, 2 * wide), BF16),
            pltpu.VMEM((b, out_rows, wide), BF16),
            pltpu.VMEM((b, out_rows, 2 * wide), BF16),
            pltpu.VMEM((b, out_rows, wide), BF16),
            pltpu.VMEM((b, out_rows, 2 * wide), BF16),
            dma((2,)),
            dma((n,)), dma((n,)),
            dma((2, n)), dma((2, n)),
            dma((n,)), dma((n,)),
            dma((b, n)), dma((b, n)),
            dma((n,)), dma((n,)),
            dma((2, nd)), dma((2, nd)),
            dma((2, b)), dma((2, b)),
        ],
        compiler_params=pltpu.CompilerParams(
            collective_id=0, has_side_effects=True, vmem_limit_bytes=56 * 1024 * 1024
        ),
        name="graph_attention_grads",
    )(
        grid_feat[0], node_feat[0], cotangent[0], w_query, w_keyval, neighbours,
        send_rows.reshape(slots, 1), send_rows.reshape(1, slots),
    )
    return d_grid[None], d_nodes[None], dw_query, dw_keyval


def solution(mesh):
    in_specs = (
        P(("groups", "dp"), "mp", None),
        P(("groups", "dp"), "mp", None),
        P(("groups", "dp"), "mp", None),
        P(),
        P(),
        P("mp", None),
        P("mp", None, None),
    )
    out_specs = (
        P(("groups", "dp"), "mp", None),
        P(("groups", "dp"), "mp", None),
        P(("groups", "mp", "dp"), None),
        P(("groups", "mp", "dp"), None),
    )
    return jax.shard_map(
        per_device, mesh=mesh, in_specs=in_specs, out_specs=out_specs, check_vma=False
    )
```

```python
import functools
import math

import jax
import jax.numpy as jnp
from jax import lax
from jax.experimental import pallas as pl
from jax.experimental.pallas import tpu as pltpu
from jax.sharding import PartitionSpec as P

HEADS = 16
LANES = 128
MESH = pl.DeviceIdType.MESH
F32 = jnp.float32
BF16 = jnp.bfloat16


def dot_nn(x, y):
    return lax.dot_general(x, y, (((1,), (0,)), ((), ())), preferred_element_type=F32)


def dot_nt(x, y):
    return lax.dot_general(x, y, (((1,), (1,)), ((), ())), preferred_element_type=F32)


def dot_tn(x, y):
    return lax.dot_general(x, y, (((0,), (0,)), ((), ())), preferred_element_type=F32)


def kernel(
    n, nd, wscale,
    gf, nf, cot, wq_h, wkv_h, nbr, sr,
    dgrid, dnodes, dwq, dwkv,
    wq, wkv, out_feat, tab, q_s, kv_s, count_s, gf_all, nf_all, dq_s, dq_all,
    part_s, ret_s, dkv_s, dkv_all, tq, tkv, rq, rkv, sq, skv, oq, okv, swq, swkv, place_s,
    local_sem, feat_ss, feat_rs, half_ss, half_rs, dq_ss, dq_rs, ret_ss, ret_rs,
    dkv_ss, dkv_rs, z_ss, z_rs, sw_ss, sw_rs,
):
    grid_dev, width = gf.shape
    nodes = nf.shape[0]
    slots = out_feat.shape[0]
    rows = slots + nodes
    cap = slots // n
    nbrs = nbr.shape[0]
    a = width // gf_all.shape[2]
    b = n // a
    high = width // a
    wide = width // b
    out_rows = dwq.shape[0]
    head = width // HEADS
    per = LANES // head
    scale = head ** (-0.5)
    me = lax.axis_index("mp")
    zd = lax.axis_index("dp")
    mine_i = me // b
    mine_j = lax.rem(me, b)

    def to_mp(src, dst, ssem, rsem, peer):
        return pltpu.make_async_remote_copy(
            src_ref=src, dst_ref=dst, send_sem=ssem, recv_sem=rsem,
            device_id={"mp": peer}, device_id_type=MESH,
        )

    def to_dp(src, dst, ssem, rsem, peer):
        return pltpu.make_async_remote_copy(
            src_ref=src, dst_ref=dst, send_sem=ssem, recv_sem=rsem,
            device_id={"dp": peer}, device_id_type=MESH,
        )

    def peer_of(o):
        return lax.rem(me + o, n)

    load_q = pltpu.make_async_copy(wq_h, wq, local_sem.at[0])
    load_kv = pltpu.make_async_copy(wkv_h, wkv, local_sem.at[1])
    load_q.start()
    load_kv.start()
    barrier = pltpu.get_barrier_semaphore()
    for o in range(1, n):
        pl.semaphore_signal(barrier, inc=1, device_id={"mp": peer_of(o)}, device_id_type=MESH)
    for o in range(1, nd):
        pl.semaphore_signal(
            barrier, inc=1, device_id={"dp": lax.rem(zd + o, nd)}, device_id_type=MESH
        )
    node_id = lax.broadcasted_iota(jnp.int32, (nodes, cap), 0)
    for p in range(n):
        place_s[:, p * cap : (p + 1) * cap] = (sr[p : p + 1, :] == node_id).astype(F32)
    place = place_s[...].astype(BF16)
    out_feat[...] = dot_tn(place, nf[...]).astype(BF16)
    tab[pl.ds(slots, nodes), :] = nf[...]
    own_slots = pl.ds(pl.multiple_of(me * cap, cap), cap)
    tab[own_slots, :] = jnp.zeros((cap, width), BF16)
    for jb in range(b):
        ret_s[jb, own_slots, :] = jnp.zeros((cap, 2 * wide), BF16)
    pl.semaphore_wait(barrier, n - 1 + nd - 1)

    feat = []
    for o in range(1, n):
        there = pl.ds(pl.multiple_of(peer_of(o) * cap, cap), cap)
        feat.append(
            to_mp(out_feat.at[there], tab.at[own_slots], feat_ss.at[o], feat_rs.at[o], peer_of(o))
        )
        feat[-1].start()

    ids = nbr[...]
    row_id = lax.broadcasted_iota(jnp.int32, (rows, grid_dev), 0)
    count = jnp.zeros((rows, grid_dev), F32)
    for k in range(nbrs):
        count += (ids[k : k + 1, :] == row_id).astype(F32)
    count = count.T
    for s in range(per):
        count_s[s * grid_dev : (s + 1) * grid_dev, :] = count
    half_cols = pl.ds(pl.multiple_of(mine_i * high, high), high)
    gf_all[me] = gf[:, half_cols]
    nf_all[me] = nf[:, half_cols]
    load_q.wait()
    q_s[...] = dot_nn(gf[...], wq[...]).astype(BF16)
    for c in feat:
        c.wait_recv()
    half = []
    for o in range(1, n):
        there = pl.ds(pl.multiple_of((peer_of(o) // b) * high, high), high)
        half.append(
            to_mp(nf.at[:, there], nf_all.at[me], half_ss.at[0, o], half_rs.at[0, o], peer_of(o))
        )
        half.append(
            to_mp(gf.at[:, there], gf_all.at[me], half_ss.at[1, o], half_rs.at[1, o], peer_of(o))
        )
    for c in half:
        c.start()
    load_kv.wait()
    kv_s[...] = dot_nn(tab[...], wkv[...]).astype(BF16)

    lane = lax.broadcasted_iota(jnp.int32, (1, LANES), 1)
    keep = [(lane // head) == s for s in range(per)]

    def spread(x):
        return jnp.concatenate([jnp.where(m, x, jnp.zeros_like(x)) for m in keep], axis=0)

    dq_copies = []
    ret_copies = []
    for jb in range(b):

        def one(blk, carry):
            off = pl.multiple_of(jb * wide + blk * LANES, LANES)
            at = pl.ds(off, LANES)
            at_v = pl.ds(pl.multiple_of(width + off, LANES), LANES)
            here = pl.ds(pl.multiple_of(blk * LANES, LANES), LANES)
            here_v = pl.ds(pl.multiple_of(wide + blk * LANES, LANES), LANES)
            qs = spread(q_s[:, at])
            cs = spread(cot[:, at])
            keys = kv_s[:, at]
            values = kv_s[:, at_v]
            times = count_s[...]
            scores = dot_nt(qs, keys) * scale
            d_attn = dot_nt(cs, values)
            top = jnp.max(
                jnp.where(times > 0, scores, -jnp.inf), axis=1, keepdims=True
            )
            e = jnp.where(times > 0, times * jnp.exp(jnp.minimum(scores - top, 0.0)), 0.0)
            attn = e / jnp.sum(e, axis=1, keepdims=True)
            ds = attn * (d_attn - jnp.sum(attn * d_attn, axis=1, keepdims=True)) * scale
            ds = ds.astype(BF16)
            attn = attn.astype(BF16)
            dq = None
            for s in range(per):
                term = dot_nn(
                    ds[s * grid_dev : (s + 1) * grid_dev],
                    jnp.where(keep[s], keys, jnp.zeros_like(keys)),
                )
                dq = term if dq is None else dq + term
            dq_s[jb, :, here] = dq.astype(BF16)
            part_s[jb, :, here] = dot_tn(ds, qs).astype(BF16)
            part_s[jb, :, here_v] = dot_tn(attn, cs).astype(BF16)
            return carry

        lax.fori_loop(0, wide // LANES, one, 0)
        for o in range(1, n):
            peer = peer_of(o)
            c = to_mp(dq_s.at[jb], dq_all.at[me], dq_ss.at[o], dq_rs.at[o], peer)

            @pl.when(lax.rem(peer, b) == jb)
            def _():
                c.start()

        for o in range(1, n):
            there = pl.ds(pl.multiple_of(peer_of(o) * cap, cap), cap)
            c = to_mp(
                part_s.at[jb, there], ret_s.at[jb, own_slots],
                ret_ss.at[jb, o], ret_rs.at[jb, o], peer_of(o),
            )
            c.start()
            ret_copies.append(c)

    dq_all[me] = dq_s[mine_j]
    acc = None
    for jb in range(b):
        term = dot_nt(dq_s[jb], wq[:, jb * wide : (jb + 1) * wide])
        acc = term if acc is None else acc + term
    dgrid[...] = acc.astype(BF16)

    for jb in range(b):
        for o in range(1, n):
            ret_copies[jb * (n - 1) + o - 1].wait_recv()
        dkv = part_s[jb, slots:, :].astype(F32) + dot_nn(place, ret_s[jb])
        dkv_s[jb] = dkv.astype(BF16)
        for o in range(1, n):
            peer = peer_of(o)
            c = to_mp(dkv_s.at[jb], dkv_all.at[me], dkv_ss.at[o], dkv_rs.at[o], peer)

            @pl.when(lax.rem(peer, b) == jb)
            def _():
                c.start()

    dkv_all[me] = dkv_s[mine_j]

    def got(src, dst, ssem, rsem):
        return to_mp(src, dst, ssem, rsem, peer_of(1))

    for c in half:
        c.wait_recv()
    for o in range(1, n):
        got(dq_s.at[0], dq_all.at[me], dq_ss.at[o], dq_rs.at[o]).wait_recv()
    term_q = dot_tn(
        gf_all[...].reshape(n * grid_dev, high), dq_all[...].reshape(n * grid_dev, wide)
    ) * wscale
    term_q = term_q.astype(BF16).reshape(b, nd, out_rows, wide)
    for d in range(nd):
        tq[d] = term_q[:, d]

    def hops(which, t, r):
        found = []
        for step in range(1, nd):
            for way in range(2):
                d = nd - step if way == 0 else step - 1
                ahead = jnp.minimum(zd + 1, nd - 1) if way == 0 else jnp.maximum(zd - 1, 0)
                c = to_dp(
                    t.at[d], r.at[way, d], z_ss.at[which, way, d], z_rs.at[which, way, d], ahead
                )
                sends = zd < d if way == 0 else zd > d
                first = zd == 0 if way == 0 else zd == nd - 1
                found.append((c, sends, first, way, d))
        return found

    def lead(found):
        for c, sends, first, way, d in found:

            @pl.when(jnp.logical_and(sends, first))
            def _():
                c.start()

    def relay(found, t, r):
        for c, sends, first, way, d in found:

            @pl.when(jnp.logical_and(sends, jnp.logical_not(first)))
            def _():
                c.wait_recv()
                t[d] = (t[d].astype(F32) + r[way, d].astype(F32)).astype(BF16)
                c.start()

    hops_q = hops(0, tq, rq)
    hops_kv = hops(1, tkv, rkv)
    lead(hops_q)

    acc = None
    for jb in range(b):
        for k in range(2):
            term = dot_nt(
                dkv_s[jb, :, k * wide : (k + 1) * wide],
                wkv[:, k * width + jb * wide : k * width + (jb + 1) * wide],
            )
            acc = term if acc is None else acc + term
    dnodes[...] = acc.astype(BF16)

    for o in range(1, n):
        got(dkv_s.at[0], dkv_all.at[me], dkv_ss.at[o], dkv_rs.at[o]).wait_recv()
    term_kv = dot_tn(
        nf_all[...].reshape(n * nodes, high), dkv_all[...].reshape(n * nodes, 2 * wide)
    ) * wscale
    term_kv = term_kv.astype(BF16).reshape(b, nd, out_rows, 2 * wide)
    for d in range(nd):
        tkv[d] = term_kv[:, d]
    lead(hops_kv)
    relay(hops_q, tq, rq)

    def finish(which, t, r, total, out, sw):
        total[...] = t[zd].astype(F32)
        for way in range(2):

            @pl.when(zd > 0 if way == 0 else zd < nd - 1)
            def _():
                to_dp(
                    t.at[0], r.at[way, zd], z_ss.at[which, way, zd], z_rs.at[which, way, zd],
                    lax.rem(zd + 1, nd),
                ).wait_recv()
                total[...] += r[way, zd].astype(F32)

        out[...] = total[...].astype(BF16)
        sent = []
        for o in range(1, b):
            mate = lax.rem(mine_j + o, b)
            c = to_mp(
                out.at[mate], sw.at[o], sw_ss.at[which, o], sw_rs.at[which, o],
                mine_i * b + mate,
            )
            c.start()
            sent.append(c)
        return sent

    sent_q = finish(0, tq, rq, sq, oq, swq)
    relay(hops_kv, tkv, rkv)
    sent_kv = finish(1, tkv, rkv, skv, okv, swkv)

    def columns(j, k):
        return pl.ds(pl.multiple_of(k * width + j * wide, LANES), wide)

    dwq[:, columns(mine_j, 0)] = oq[mine_j]
    for o in range(1, b):
        source = lax.rem(mine_j + b - o, b)
        sent_q[o - 1].wait_recv()
        dwq[:, columns(source, 0)] = swq[o]
    for k in range(2):
        dwkv[:, columns(mine_j, k)] = okv[mine_j][:, k * wide : (k + 1) * wide]
    for o in range(1, b):
        source = lax.rem(mine_j + b - o, b)
        sent_kv[o - 1].wait_recv()
        for k in range(2):
            dwkv[:, columns(source, k)] = swkv[o][:, k * wide : (k + 1) * wide]

    for c in feat + half + ret_copies + sent_q + sent_kv:
        c.wait_send()
    for c, sends, first, way, d in hops_q + hops_kv:

        @pl.when(sends)
        def _():
            c.wait_send()

    for o in range(1, n):
        got(dq_s.at[0], dq_all.at[me], dq_ss.at[o], dq_rs.at[o]).wait_send()
        got(dkv_s.at[0], dkv_all.at[me], dkv_ss.at[o], dkv_rs.at[o]).wait_send()


def write_out(d_grid, d_nodes, dw_query, dw_keyval, out_grid, out_nodes, out_q, out_kv):
    out_grid[...] = d_grid[...]
    out_nodes[...] = d_nodes[...]
    out_q[...] = dw_query[...].astype(F32)
    out_kv[...] = dw_keyval[...].astype(F32)


def per_device(grid_feat, node_feat, cotangent, w_query, w_keyval, neighbours, send_rows):
    n = lax.axis_size("mp")
    nd = lax.axis_size("dp")
    samples_dev, grid_dev, width = grid_feat.shape
    nodes = node_feat.shape[1]
    cap = send_rows.shape[2]
    slots = n * cap
    rows = slots + nodes
    a = 2
    b = n // a
    high = width // a
    wide = width // b
    out_rows = width // (n * nd)
    per = LANES * HEADS // width
    wscale = 1.0 / math.sqrt(samples_dev * nd * grid_dev * n)
    vmem = pl.BlockSpec(memory_space=pltpu.VMEM)
    anywhere = pl.BlockSpec(memory_space=pl.ANY)
    dma = pltpu.SemaphoreType.DMA
    d_grid, d_nodes, dw_query, dw_keyval = pl.pallas_call(
        functools.partial(kernel, n, nd, wscale),
        out_shape=(
            jax.ShapeDtypeStruct((grid_dev, width), BF16),
            jax.ShapeDtypeStruct((nodes, width), BF16),
            jax.ShapeDtypeStruct((out_rows, width), BF16),
            jax.ShapeDtypeStruct((out_rows, 2 * width), BF16),
        ),
        in_specs=[vmem, vmem, vmem, anywhere, anywhere, vmem, vmem],
        out_specs=(vmem, vmem, vmem, vmem),
        scratch_shapes=[
            pltpu.VMEM((width, width), BF16),
            pltpu.VMEM((width, 2 * width), BF16),
            pltpu.VMEM((slots, width), BF16),
            pltpu.VMEM((rows, width), BF16),
            pltpu.VMEM((grid_dev, width), BF16),
            pltpu.VMEM((rows, 2 * width), BF16),
            pltpu.VMEM((per * grid_dev, rows), F32),
            pltpu.VMEM((n, grid_dev, high), BF16),
            pltpu.VMEM((n, nodes, high), BF16),
            pltpu.VMEM((b, grid_dev, wide), BF16),
            pltpu.VMEM((n, grid_dev, wide), BF16),
            pltpu.VMEM((b, rows, 2 * wide), BF16),
            pltpu.VMEM((b, slots, 2 * wide), BF16),
            pltpu.VMEM((b, nodes, 2 * wide), BF16),
            pltpu.VMEM((n, nodes, 2 * wide), BF16),
            pltpu.VMEM((nd, b, out_rows, wide), BF16),
            pltpu.VMEM((nd, b, out_rows, 2 * wide), BF16),
            pltpu.VMEM((2, nd, b, out_rows, wide), BF16),
            pltpu.VMEM((2, nd, b, out_rows, 2 * wide), BF16),
            pltpu.VMEM((b, out_rows, wide), F32),
            pltpu.VMEM((b, out_rows, 2 * wide), F32),
            pltpu.VMEM((b, out_rows, wide), BF16),
            pltpu.VMEM((b, out_rows, 2 * wide), BF16),
            pltpu.VMEM((b, out_rows, wide), BF16),
            pltpu.VMEM((b, out_rows, 2 * wide), BF16),
            pltpu.VMEM((nodes, slots), F32),
            dma((2,)),
            dma((n,)), dma((n,)),
            dma((2, n)), dma((2, n)),
            dma((n,)), dma((n,)),
            dma((b, n)), dma((b, n)),
            dma((n,)), dma((n,)),
            dma((2, 2, nd)), dma((2, 2, nd)),
            dma((2, b)), dma((2, b)),
        ],
        compiler_params=pltpu.CompilerParams(
            collective_id=0, has_side_effects=True, vmem_limit_bytes=56 * 1024 * 1024
        ),
        name="graph_attention_grads",
    )(
        grid_feat[0], node_feat[0], cotangent[0], w_query, w_keyval, neighbours.T, send_rows[0],
    )
    d_grid, d_nodes, dw_query, dw_keyval = pl.pallas_call(
        write_out,
        out_shape=(
            jax.ShapeDtypeStruct((grid_dev, width), BF16),
            jax.ShapeDtypeStruct((nodes, width), BF16),
            jax.ShapeDtypeStruct((out_rows, width), F32),
            jax.ShapeDtypeStruct((out_rows, 2 * width), F32),
        ),
        in_specs=[vmem, vmem, vmem, vmem],
        out_specs=(vmem, vmem, vmem, vmem),
        name="write_out",
    )(d_grid, d_nodes, dw_query, dw_keyval)
    return d_grid[None], d_nodes[None], dw_query, dw_keyval


def solution(mesh):
    in_specs = (
        P(("groups", "dp"), "mp", None),
        P(("groups", "dp"), "mp", None),
        P(("groups", "dp"), "mp", None),
        P(),
        P(),
        P("mp", None),
        P("mp", None, None),
    )
    out_specs = (
        P(("groups", "dp"), "mp", None),
        P(("groups", "dp"), "mp", None),
        P(("groups", "mp", "dp"), None),
        P(("groups", "mp", "dp"), None),
    )
    return jax.shard_map(
        per_device, mesh=mesh, in_specs=in_specs, out_specs=out_specs, check_vma=False
    )
```

```python
import functools
import math

import jax
import jax.numpy as jnp
from jax import lax
from jax.experimental import pallas as pl
from jax.experimental.pallas import tpu as pltpu
from jax.sharding import PartitionSpec as P

HEADS = 16
LANES = 128
MESH = pl.DeviceIdType.MESH
F32 = jnp.float32
BF16 = jnp.bfloat16


def dot_nn(x, y):
    return lax.dot_general(x, y, (((1,), (0,)), ((), ())), preferred_element_type=F32)


def dot_nt(x, y):
    return lax.dot_general(x, y, (((1,), (1,)), ((), ())), preferred_element_type=F32)


def dot_tn(x, y):
    return lax.dot_general(x, y, (((0,), (0,)), ((), ())), preferred_element_type=F32)


def kernel(
    n, nd, wscale,
    gf, nf, cot, wq_h, wkv_h, nbr, sr,
    dgrid, dnodes, dwq, dwkv,
    wq, wkv, out_feat, tab, q_s, kv_s, count_s, gf_all, nf_all, dq_s, dq_all,
    part_s, ret_s, dkv_s, dkv_all, tq, tkv, rq, rkv, sq, skv, oq, okv, swq, swkv, place_s,
    local_sem, feat_ss, feat_rs, half_ss, half_rs, dq_ss, dq_rs, ret_ss, ret_rs,
    dkv_ss, dkv_rs, z_ss, z_rs, sw_ss, sw_rs,
):
    grid_dev, width = gf.shape
    nodes = nf.shape[0]
    slots = out_feat.shape[0]
    rows = slots + nodes
    cap = slots // n
    nbrs = nbr.shape[0]
    a = width // gf_all.shape[2]
    b = n // a
    high = width // a
    wide = width // b
    out_rows = dwq.shape[0]
    head = width // HEADS
    per = LANES // head
    scale = head ** (-0.5)
    me = lax.axis_index("mp")
    zd = lax.axis_index("dp")
    mine_i = me // b
    mine_j = lax.rem(me, b)

    def to_mp(src, dst, ssem, rsem, peer):
        return pltpu.make_async_remote_copy(
            src_ref=src, dst_ref=dst, send_sem=ssem, recv_sem=rsem,
            device_id={"mp": peer}, device_id_type=MESH,
        )

    def to_dp(src, dst, ssem, rsem, peer):
        return pltpu.make_async_remote_copy(
            src_ref=src, dst_ref=dst, send_sem=ssem, recv_sem=rsem,
            device_id={"dp": peer}, device_id_type=MESH,
        )

    def peer_of(o):
        return lax.rem(me + o, n)

    load_q = pltpu.make_async_copy(wq_h, wq, local_sem.at[0])
    load_kv = pltpu.make_async_copy(wkv_h, wkv, local_sem.at[1])
    load_q.start()
    load_kv.start()
    barrier = pltpu.get_barrier_semaphore()
    for o in range(1, n):
        pl.semaphore_signal(barrier, inc=1, device_id={"mp": peer_of(o)}, device_id_type=MESH)
    for o in range(1, nd):
        pl.semaphore_signal(
            barrier, inc=1, device_id={"dp": lax.rem(zd + o, nd)}, device_id_type=MESH
        )
    node_id = lax.broadcasted_iota(jnp.int32, (nodes, cap), 0)
    for p in range(n):
        place_s[:, p * cap : (p + 1) * cap] = (sr[p : p + 1, :] == node_id).astype(F32)
    place = place_s[...].astype(BF16)
    out_feat[...] = dot_tn(place, nf[...]).astype(BF16)
    tab[pl.ds(slots, nodes), :] = nf[...]
    own_slots = pl.ds(pl.multiple_of(me * cap, cap), cap)
    tab[own_slots, :] = jnp.zeros((cap, width), BF16)
    for jb in range(b):
        ret_s[jb, own_slots, :] = jnp.zeros((cap, 2 * wide), BF16)
    pl.semaphore_wait(barrier, n - 1 + nd - 1)

    feat = []
    for o in range(1, n):
        there = pl.ds(pl.multiple_of(peer_of(o) * cap, cap), cap)
        feat.append(
            to_mp(out_feat.at[there], tab.at[own_slots], feat_ss.at[o], feat_rs.at[o], peer_of(o))
        )
        feat[-1].start()
    half = []
    for which, whole, parts in ((1, gf, gf_all), (0, nf, nf_all)):
        for o in range(1, n):
            there = pl.ds(pl.multiple_of((peer_of(o) // b) * high, high), high)
            half.append(
                to_mp(
                    whole.at[:, there], parts.at[me],
                    half_ss.at[which, o], half_rs.at[which, o], peer_of(o),
                )
            )
            half[-1].start()
    half_cols = pl.ds(pl.multiple_of(mine_i * high, high), high)
    gf_all[me] = gf[:, half_cols]
    nf_all[me] = nf[:, half_cols]

    ids = nbr[...]
    row_id = lax.broadcasted_iota(jnp.int32, (rows, grid_dev), 0)
    count = jnp.zeros((rows, grid_dev), F32)
    for k in range(nbrs):
        count += (ids[k : k + 1, :] == row_id).astype(F32)
    count = count.T
    for s in range(per):
        count_s[s * grid_dev : (s + 1) * grid_dev, :] = count
    load_q.wait()
    q_s[...] = dot_nn(gf[...], wq[...]).astype(BF16)
    for c in feat:
        c.wait_recv()
    load_kv.wait()
    kv_s[...] = dot_nn(tab[...], wkv[...]).astype(BF16)

    lane = lax.broadcasted_iota(jnp.int32, (1, LANES), 1)
    keep = [(lane // head) == s for s in range(per)]

    def spread(x):
        return jnp.concatenate([jnp.where(m, x, jnp.zeros_like(x)) for m in keep], axis=0)

    dq_copies = []
    ret_copies = []
    for jb in range(b):

        def one(blk, carry):
            off = pl.multiple_of(jb * wide + blk * LANES, LANES)
            at = pl.ds(off, LANES)
            at_v = pl.ds(pl.multiple_of(width + off, LANES), LANES)
            here = pl.ds(pl.multiple_of(blk * LANES, LANES), LANES)
            here_v = pl.ds(pl.multiple_of(wide + blk * LANES, LANES), LANES)
            qs = spread(q_s[:, at])
            cs = spread(cot[:, at])
            keys = kv_s[:, at]
            values = kv_s[:, at_v]
            times = count_s[...]
            scores = dot_nt(qs, keys) * scale
            d_attn = dot_nt(cs, values)
            top = jnp.max(
                jnp.where(times > 0, scores, -jnp.inf), axis=1, keepdims=True
            )
            e = jnp.where(times > 0, times * jnp.exp(jnp.minimum(scores - top, 0.0)), 0.0)
            attn = e / jnp.sum(e, axis=1, keepdims=True)
            ds = attn * (d_attn - jnp.sum(attn * d_attn, axis=1, keepdims=True)) * scale
            ds = ds.astype(BF16)
            attn = attn.astype(BF16)
            dq = None
            for s in range(per):
                term = dot_nn(
                    ds[s * grid_dev : (s + 1) * grid_dev],
                    jnp.where(keep[s], keys, jnp.zeros_like(keys)),
                )
                dq = term if dq is None else dq + term
            dq_s[jb, :, here] = dq.astype(BF16)
            part_s[jb, :, here] = dot_tn(ds, qs).astype(BF16)
            part_s[jb, :, here_v] = dot_tn(attn, cs).astype(BF16)
            return carry

        lax.fori_loop(0, wide // LANES, one, 0)
        for o in range(1, n):
            there = pl.ds(pl.multiple_of(peer_of(o) * cap, cap), cap)
            c = to_mp(
                part_s.at[jb, there], ret_s.at[jb, own_slots],
                ret_ss.at[jb, o], ret_rs.at[jb, o], peer_of(o),
            )
            c.start()
            ret_copies.append(c)
        for o in range(1, n):
            peer = peer_of(o)
            c = to_mp(dq_s.at[jb], dq_all.at[me], dq_ss.at[o], dq_rs.at[o], peer)

            @pl.when(lax.rem(peer, b) == jb)
            def _():
                c.start()

    dq_all[me] = dq_s[mine_j]
    for jb in range(b):
        for o in range(1, n):
            ret_copies[jb * (n - 1) + o - 1].wait_recv()
        dkv = part_s[jb, slots:, :].astype(F32) + dot_nn(place, ret_s[jb])
        dkv_s[jb] = dkv.astype(BF16)
        for o in range(1, n):
            peer = peer_of(o)
            c = to_mp(dkv_s.at[jb], dkv_all.at[me], dkv_ss.at[o], dkv_rs.at[o], peer)

            @pl.when(lax.rem(peer, b) == jb)
            def _():
                c.start()

    dkv_all[me] = dkv_s[mine_j]

    acc = None
    for jb in range(b):
        term = dot_nt(dq_s[jb], wq[:, jb * wide : (jb + 1) * wide])
        acc = term if acc is None else acc + term
    dgrid[...] = acc.astype(BF16)

    def got(src, dst, ssem, rsem):
        return to_mp(src, dst, ssem, rsem, peer_of(1))

    for c in half:
        c.wait_recv()
    for o in range(1, n):
        got(dq_s.at[0], dq_all.at[me], dq_ss.at[o], dq_rs.at[o]).wait_recv()
    term_q = dot_tn(
        gf_all[...].reshape(n * grid_dev, high), dq_all[...].reshape(n * grid_dev, wide)
    ) * wscale
    term_q = term_q.astype(BF16).reshape(b, nd, out_rows, wide)
    for d in range(nd):
        tq[d] = term_q[:, d]

    far = nd // 2

    def region(k, way):
        if 2 * k == nd:
            return slice(0, b // 2) if way == 0 else slice(b // 2, b)
        return slice(0, b)

    def hops(which, t, r):
        found = {}
        for k in range(far, 0, -1):
            for way in range(2):
                d = lax.rem(zd + k, nd) if way == 0 else lax.rem(zd + nd - k, nd)
                ahead = lax.rem(zd + 1, nd) if way == 0 else lax.rem(zd + nd - 1, nd)
                piece = region(k, way)
                found[k, way] = (
                    to_dp(
                        t.at[d, piece], r.at[way, k, piece],
                        z_ss.at[which, way, k], z_rs.at[which, way, k], ahead,
                    ),
                    d,
                )
        return found

    def lead(found):
        for way in range(2):
            found[far, way][0].start()

    def relay(found, t, r):
        for k in range(far - 1, 0, -1):
            for way in range(2):
                c, d = found[k, way]
                found[k + 1, way][0].wait_recv()
                piece = region(k + 1, way)
                t[d, piece] = (t[d, piece].astype(F32) + r[way, k + 1, piece].astype(F32)).astype(
                    BF16
                )
                c.start()

    hops_q = hops(0, tq, rq)
    hops_kv = hops(1, tkv, rkv)
    lead(hops_q)

    acc = None
    for jb in range(b):
        for k in range(2):
            term = dot_nt(
                dkv_s[jb, :, k * wide : (k + 1) * wide],
                wkv[:, k * width + jb * wide : k * width + (jb + 1) * wide],
            )
            acc = term if acc is None else acc + term
    dnodes[...] = acc.astype(BF16)

    relay(hops_q, tq, rq)
    for o in range(1, n):
        got(dkv_s.at[0], dkv_all.at[me], dkv_ss.at[o], dkv_rs.at[o]).wait_recv()
    term_kv = dot_tn(
        nf_all[...].reshape(n * nodes, high), dkv_all[...].reshape(n * nodes, 2 * wide)
    ) * wscale
    term_kv = term_kv.astype(BF16).reshape(b, nd, out_rows, 2 * wide)
    for d in range(nd):
        tkv[d] = term_kv[:, d]
    lead(hops_kv)

    def finish(which, found, t, r, total, out, sw):
        total[...] = t[zd].astype(F32)
        for way in range(2):
            found[1, way][0].wait_recv()
            piece = region(1, way)
            total[piece] += r[way, 1, piece].astype(F32)
        out[...] = total[...].astype(BF16)
        sent = []
        for o in range(1, b):
            mate = lax.rem(mine_j + o, b)
            c = to_mp(
                out.at[mate], sw.at[o], sw_ss.at[which, o], sw_rs.at[which, o],
                mine_i * b + mate,
            )
            c.start()
            sent.append(c)
        return sent

    sent_q = finish(0, hops_q, tq, rq, sq, oq, swq)
    relay(hops_kv, tkv, rkv)
    sent_kv = finish(1, hops_kv, tkv, rkv, skv, okv, swkv)

    def columns(j, k):
        return pl.ds(pl.multiple_of(k * width + j * wide, LANES), wide)

    dwq[:, columns(mine_j, 0)] = oq[mine_j]
    for o in range(1, b):
        source = lax.rem(mine_j + b - o, b)
        sent_q[o - 1].wait_recv()
        dwq[:, columns(source, 0)] = swq[o]
    for k in range(2):
        dwkv[:, columns(mine_j, k)] = okv[mine_j][:, k * wide : (k + 1) * wide]
    for o in range(1, b):
        source = lax.rem(mine_j + b - o, b)
        sent_kv[o - 1].wait_recv()
        for k in range(2):
            dwkv[:, columns(source, k)] = swkv[o][:, k * wide : (k + 1) * wide]

    for c in feat + half + ret_copies + sent_q + sent_kv:
        c.wait_send()
    for c, _ in list(hops_q.values()) + list(hops_kv.values()):
        c.wait_send()
    for o in range(1, n):
        got(dq_s.at[0], dq_all.at[me], dq_ss.at[o], dq_rs.at[o]).wait_send()
        got(dkv_s.at[0], dkv_all.at[me], dkv_ss.at[o], dkv_rs.at[o]).wait_send()


def write_out(d_grid, d_nodes, dw_query, dw_keyval, out_grid, out_nodes, out_q, out_kv):
    out_grid[...] = d_grid[...]
    out_nodes[...] = d_nodes[...]
    out_q[...] = dw_query[...].astype(F32)
    out_kv[...] = dw_keyval[...].astype(F32)


def per_device(grid_feat, node_feat, cotangent, w_query, w_keyval, neighbours, send_rows):
    n = lax.axis_size("mp")
    nd = lax.axis_size("dp")
    samples_dev, grid_dev, width = grid_feat.shape
    nodes = node_feat.shape[1]
    cap = send_rows.shape[2]
    slots = n * cap
    rows = slots + nodes
    a = 2
    b = n // a
    high = width // a
    wide = width // b
    out_rows = width // (n * nd)
    per = LANES * HEADS // width
    wscale = 1.0 / math.sqrt(samples_dev * nd * grid_dev * n)
    vmem = pl.BlockSpec(memory_space=pltpu.VMEM)
    anywhere = pl.BlockSpec(memory_space=pl.ANY)
    dma = pltpu.SemaphoreType.DMA
    d_grid, d_nodes, dw_query, dw_keyval = pl.pallas_call(
        functools.partial(kernel, n, nd, wscale),
        out_shape=(
            jax.ShapeDtypeStruct((grid_dev, width), BF16),
            jax.ShapeDtypeStruct((nodes, width), BF16),
            jax.ShapeDtypeStruct((out_rows, width), BF16),
            jax.ShapeDtypeStruct((out_rows, 2 * width), BF16),
        ),
        in_specs=[vmem, vmem, vmem, anywhere, anywhere, vmem, vmem],
        out_specs=(vmem, vmem, vmem, vmem),
        scratch_shapes=[
            pltpu.VMEM((width, width), BF16),
            pltpu.VMEM((width, 2 * width), BF16),
            pltpu.VMEM((slots, width), BF16),
            pltpu.VMEM((rows, width), BF16),
            pltpu.VMEM((grid_dev, width), BF16),
            pltpu.VMEM((rows, 2 * width), BF16),
            pltpu.VMEM((per * grid_dev, rows), F32),
            pltpu.VMEM((n, grid_dev, high), BF16),
            pltpu.VMEM((n, nodes, high), BF16),
            pltpu.VMEM((b, grid_dev, wide), BF16),
            pltpu.VMEM((n, grid_dev, wide), BF16),
            pltpu.VMEM((b, rows, 2 * wide), BF16),
            pltpu.VMEM((b, slots, 2 * wide), BF16),
            pltpu.VMEM((b, nodes, 2 * wide), BF16),
            pltpu.VMEM((n, nodes, 2 * wide), BF16),
            pltpu.VMEM((nd, b, out_rows, wide), BF16),
            pltpu.VMEM((nd, b, out_rows, 2 * wide), BF16),
            pltpu.VMEM((2, nd // 2 + 1, b, out_rows, wide), BF16),
            pltpu.VMEM((2, nd // 2 + 1, b, out_rows, 2 * wide), BF16),
            pltpu.VMEM((b, out_rows, wide), F32),
            pltpu.VMEM((b, out_rows, 2 * wide), F32),
            pltpu.VMEM((b, out_rows, wide), BF16),
            pltpu.VMEM((b, out_rows, 2 * wide), BF16),
            pltpu.VMEM((b, out_rows, wide), BF16),
            pltpu.VMEM((b, out_rows, 2 * wide), BF16),
            pltpu.VMEM((nodes, slots), F32),
            dma((2,)),
            dma((n,)), dma((n,)),
            dma((2, n)), dma((2, n)),
            dma((n,)), dma((n,)),
            dma((b, n)), dma((b, n)),
            dma((n,)), dma((n,)),
            dma((2, 2, nd // 2 + 1)), dma((2, 2, nd // 2 + 1)),
            dma((2, b)), dma((2, b)),
        ],
        compiler_params=pltpu.CompilerParams(
            collective_id=0, has_side_effects=True, vmem_limit_bytes=56 * 1024 * 1024
        ),
        name="graph_attention_grads",
    )(
        grid_feat[0], node_feat[0], cotangent[0], w_query, w_keyval, neighbours.T, send_rows[0],
    )
    d_grid, d_nodes, dw_query, dw_keyval = pl.pallas_call(
        write_out,
        out_shape=(
            jax.ShapeDtypeStruct((grid_dev, width), BF16),
            jax.ShapeDtypeStruct((nodes, width), BF16),
            jax.ShapeDtypeStruct((out_rows, width), F32),
            jax.ShapeDtypeStruct((out_rows, 2 * width), F32),
        ),
        in_specs=[vmem, vmem, vmem, vmem],
        out_specs=(vmem, vmem, vmem, vmem),
        name="write_out",
    )(d_grid, d_nodes, dw_query, dw_keyval)
    return d_grid[None], d_nodes[None], dw_query, dw_keyval


def solution(mesh):
    in_specs = (
        P(("groups", "dp"), "mp", None),
        P(("groups", "dp"), "mp", None),
        P(("groups", "dp"), "mp", None),
        P(),
        P(),
        P("mp", None),
        P("mp", None, None),
    )
    out_specs = (
        P(("groups", "dp"), "mp", None),
        P(("groups", "dp"), "mp", None),
        P(("groups", "mp", "dp"), None),
        P(("groups", "mp", "dp"), None),
    )
    return jax.shard_map(
        per_device, mesh=mesh, in_specs=in_specs, out_specs=out_specs, check_vma=False
    )
```

```python
import functools
import math

import jax
import jax.numpy as jnp
from jax import lax
from jax.experimental import pallas as pl
from jax.experimental.pallas import tpu as pltpu
from jax.sharding import PartitionSpec as P

HEADS = 16
LANES = 128
MESH = pl.DeviceIdType.MESH
F32 = jnp.float32
BF16 = jnp.bfloat16


def dot_nn(x, y):
    return lax.dot_general(x, y, (((1,), (0,)), ((), ())), preferred_element_type=F32)


def dot_nt(x, y):
    return lax.dot_general(x, y, (((1,), (1,)), ((), ())), preferred_element_type=F32)


def dot_tn(x, y):
    return lax.dot_general(x, y, (((0,), (0,)), ((), ())), preferred_element_type=F32)


def kernel(
    n, nd, wscale,
    gf, nf, cot, wq_h, wkv_h, nbr, sr,
    dgrid, dnodes, dwq, dwkv,
    wq, wkv, out_feat, tab, q_s, kv_s, count_s, gf_all, nf_all, dq_s, dq_all,
    part_s, ret_s, dkv_s, dkv_all, tq, tkv, rq, rkv, sq, skv, oq, okv, swq, swkv, place_s,
    local_sem, feat_ss, feat_rs, half_ss, half_rs, dq_ss, dq_rs, ret_ss, ret_rs,
    dkv_ss, dkv_rs, z_ss, z_rs, sw_ss, sw_rs,
):
    grid_dev, width = gf.shape
    nodes = nf.shape[0]
    slots = out_feat.shape[0]
    rows = slots + nodes
    cap = slots // n
    nbrs = nbr.shape[0]
    a = width // gf_all.shape[2]
    b = n // a
    high = width // a
    wide = width // b
    out_rows = dwq.shape[0]
    head = width // HEADS
    per = LANES // head
    scale = head ** (-0.5)
    me = lax.axis_index("mp")
    zd = lax.axis_index("dp")
    mine_i = me // b
    mine_j = lax.rem(me, b)

    def to_mp(src, dst, ssem, rsem, peer):
        return pltpu.make_async_remote_copy(
            src_ref=src, dst_ref=dst, send_sem=ssem, recv_sem=rsem,
            device_id={"mp": peer}, device_id_type=MESH,
        )

    def to_dp(src, dst, ssem, rsem, peer):
        return pltpu.make_async_remote_copy(
            src_ref=src, dst_ref=dst, send_sem=ssem, recv_sem=rsem,
            device_id={"dp": peer}, device_id_type=MESH,
        )

    def peer_of(o):
        return lax.rem(me + o, n)

    load_q = pltpu.make_async_copy(wq_h, wq, local_sem.at[0])
    load_kv = pltpu.make_async_copy(wkv_h, wkv, local_sem.at[1])
    load_q.start()
    load_kv.start()
    barrier = pltpu.get_barrier_semaphore()
    for o in range(1, n):
        pl.semaphore_signal(barrier, inc=1, device_id={"mp": peer_of(o)}, device_id_type=MESH)
    for o in range(1, nd):
        pl.semaphore_signal(
            barrier, inc=1, device_id={"dp": lax.rem(zd + o, nd)}, device_id_type=MESH
        )
    node_id = lax.broadcasted_iota(jnp.int32, (nodes, cap), 0)
    for p in range(n):
        place_s[:, p * cap : (p + 1) * cap] = (sr[p : p + 1, :] == node_id).astype(F32)
    place = place_s[...].astype(BF16)
    out_feat[...] = dot_tn(place, nf[...]).astype(BF16)
    tab[pl.ds(slots, nodes), :] = nf[...]
    own_slots = pl.ds(pl.multiple_of(me * cap, cap), cap)
    tab[own_slots, :] = jnp.zeros((cap, width), BF16)
    for jb in range(b):
        ret_s[jb, own_slots, :] = jnp.zeros((cap, 2 * wide), BF16)
    pl.semaphore_wait(barrier, n - 1 + nd - 1)

    feat = []
    for o in range(1, n):
        there = pl.ds(pl.multiple_of(peer_of(o) * cap, cap), cap)
        feat.append(
            to_mp(out_feat.at[there], tab.at[own_slots], feat_ss.at[o], feat_rs.at[o], peer_of(o))
        )
        feat[-1].start()
    half_cols = pl.ds(pl.multiple_of(mine_i * high, high), high)
    other_i = lax.rem(mine_i + 1, a)
    across = other_i * b + mine_j
    other_cols = pl.ds(pl.multiple_of(other_i * high, high), high)
    feature_sets = ((1, gf, gf_all), (0, nf, nf_all))

    def mate_of(o):
        return mine_i * b + lax.rem(mine_j + o, b)

    crossing = []
    half = []
    for which, whole, parts in feature_sets:
        crossing.append(
            to_mp(
                whole.at[:, other_cols], parts.at[me],
                half_ss.at[which, 0], half_rs.at[which, 0], across,
            )
        )
        crossing[-1].start()
        for o in range(1, b):
            half.append(
                to_mp(
                    whole.at[:, half_cols], parts.at[me],
                    half_ss.at[which, o], half_rs.at[which, o], mate_of(o),
                )
            )
            half[-1].start()
    gf_all[me] = gf[:, half_cols]
    nf_all[me] = nf[:, half_cols]

    ids = nbr[...]
    row_id = lax.broadcasted_iota(jnp.int32, (rows, grid_dev), 0)
    count = jnp.zeros((rows, grid_dev), F32)
    for k in range(nbrs):
        count += (ids[k : k + 1, :] == row_id).astype(F32)
    count = count.T
    for s in range(per):
        count_s[s * grid_dev : (s + 1) * grid_dev, :] = count
    load_q.wait()
    q_s[...] = dot_nn(gf[...], wq[...]).astype(BF16)
    for c in feat:
        c.wait_recv()
    load_kv.wait()
    kv_s[...] = dot_nn(tab[...], wkv[...]).astype(BF16)

    lane = lax.broadcasted_iota(jnp.int32, (1, LANES), 1)
    keep = [(lane // head) == s for s in range(per)]

    def spread(x):
        return jnp.concatenate([jnp.where(m, x, jnp.zeros_like(x)) for m in keep], axis=0)

    dq_copies = []
    ret_copies = []
    for jb in range(b):

        def one(blk, carry):
            off = pl.multiple_of(jb * wide + blk * LANES, LANES)
            at = pl.ds(off, LANES)
            at_v = pl.ds(pl.multiple_of(width + off, LANES), LANES)
            here = pl.ds(pl.multiple_of(blk * LANES, LANES), LANES)
            here_v = pl.ds(pl.multiple_of(wide + blk * LANES, LANES), LANES)
            qs = spread(q_s[:, at])
            cs = spread(cot[:, at])
            keys = kv_s[:, at]
            values = kv_s[:, at_v]
            times = count_s[...]
            scores = dot_nt(qs, keys) * scale
            d_attn = dot_nt(cs, values)
            top = jnp.max(
                jnp.where(times > 0, scores, -jnp.inf), axis=1, keepdims=True
            )
            e = jnp.where(times > 0, times * jnp.exp(jnp.minimum(scores - top, 0.0)), 0.0)
            attn = e / jnp.sum(e, axis=1, keepdims=True)
            ds = attn * (d_attn - jnp.sum(attn * d_attn, axis=1, keepdims=True)) * scale
            ds = ds.astype(BF16)
            attn = attn.astype(BF16)
            dq = None
            for s in range(per):
                term = dot_nn(
                    ds[s * grid_dev : (s + 1) * grid_dev],
                    jnp.where(keep[s], keys, jnp.zeros_like(keys)),
                )
                dq = term if dq is None else dq + term
            dq_s[jb, :, here] = dq.astype(BF16)
            part_s[jb, :, here] = dot_tn(ds, qs).astype(BF16)
            part_s[jb, :, here_v] = dot_tn(attn, cs).astype(BF16)
            return carry

        lax.fori_loop(0, wide // LANES, one, 0)
        if jb == 0:
            for c, (which, whole, parts) in zip(crossing, feature_sets):
                c.wait_recv()
                for o in range(1, b):
                    half.append(
                        to_mp(
                            parts.at[across], parts.at[across],
                            half_ss.at[which, b + o], half_rs.at[which, b + o], mate_of(o),
                        )
                    )
                    half[-1].start()
        for o in range(1, n):
            there = pl.ds(pl.multiple_of(peer_of(o) * cap, cap), cap)
            c = to_mp(
                part_s.at[jb, there], ret_s.at[jb, own_slots],
                ret_ss.at[jb, o], ret_rs.at[jb, o], peer_of(o),
            )
            c.start()
            ret_copies.append(c)
        for o in range(1, n):
            peer = peer_of(o)
            c = to_mp(dq_s.at[jb], dq_all.at[me], dq_ss.at[o], dq_rs.at[o], peer)

            @pl.when(lax.rem(peer, b) == jb)
            def _():
                c.start()

    dq_all[me] = dq_s[mine_j]
    for jb in range(b):
        for o in range(1, n):
            ret_copies[jb * (n - 1) + o - 1].wait_recv()
        dkv = part_s[jb, slots:, :].astype(F32) + dot_nn(place, ret_s[jb])
        dkv_s[jb] = dkv.astype(BF16)
        for o in range(1, n):
            peer = peer_of(o)
            c = to_mp(dkv_s.at[jb], dkv_all.at[me], dkv_ss.at[o], dkv_rs.at[o], peer)

            @pl.when(lax.rem(peer, b) == jb)
            def _():
                c.start()

    dkv_all[me] = dkv_s[mine_j]

    acc = None
    for jb in range(b):
        term = dot_nt(dq_s[jb], wq[:, jb * wide : (jb + 1) * wide])
        acc = term if acc is None else acc + term
    dgrid[...] = acc.astype(BF16)

    def got(src, dst, ssem, rsem):
        return to_mp(src, dst, ssem, rsem, peer_of(1))

    for c in half:
        c.wait_recv()
    for o in range(1, n):
        got(dq_s.at[0], dq_all.at[me], dq_ss.at[o], dq_rs.at[o]).wait_recv()
    term_q = dot_tn(
        gf_all[...].reshape(n * grid_dev, high), dq_all[...].reshape(n * grid_dev, wide)
    ) * wscale
    term_q = term_q.astype(BF16).reshape(b, nd, out_rows, wide)
    for d in range(nd):
        tq[d] = term_q[:, d]

    far = nd // 2

    def region(k, way):
        if 2 * k == nd:
            return slice(0, b // 2) if way == 0 else slice(b // 2, b)
        return slice(0, b)

    def hops(which, t, r):
        found = {}
        for k in range(far, 0, -1):
            for way in range(2):
                d = lax.rem(zd + k, nd) if way == 0 else lax.rem(zd + nd - k, nd)
                ahead = lax.rem(zd + 1, nd) if way == 0 else lax.rem(zd + nd - 1, nd)
                piece = region(k, way)
                found[k, way] = (
                    to_dp(
                        t.at[d, piece], r.at[way, k, piece],
                        z_ss.at[which, way, k], z_rs.at[which, way, k], ahead,
                    ),
                    d,
                )
        return found

    def lead(found):
        for way in range(2):
            found[far, way][0].start()

    def relay(found, t, r):
        for k in range(far - 1, 0, -1):
            for way in range(2):
                c, d = found[k, way]
                found[k + 1, way][0].wait_recv()
                piece = region(k + 1, way)
                t[d, piece] = (t[d, piece].astype(F32) + r[way, k + 1, piece].astype(F32)).astype(
                    BF16
                )
                c.start()

    hops_q = hops(0, tq, rq)
    hops_kv = hops(1, tkv, rkv)
    lead(hops_q)

    acc = None
    for jb in range(b):
        for k in range(2):
            term = dot_nt(
                dkv_s[jb, :, k * wide : (k + 1) * wide],
                wkv[:, k * width + jb * wide : k * width + (jb + 1) * wide],
            )
            acc = term if acc is None else acc + term
    dnodes[...] = acc.astype(BF16)

    relay(hops_q, tq, rq)
    for o in range(1, n):
        got(dkv_s.at[0], dkv_all.at[me], dkv_ss.at[o], dkv_rs.at[o]).wait_recv()
    term_kv = dot_tn(
        nf_all[...].reshape(n * nodes, high), dkv_all[...].reshape(n * nodes, 2 * wide)
    ) * wscale
    term_kv = term_kv.astype(BF16).reshape(b, nd, out_rows, 2 * wide)
    for d in range(nd):
        tkv[d] = term_kv[:, d]
    lead(hops_kv)

    def finish(which, found, t, r, total, out, sw):
        total[...] = t[zd].astype(F32)
        for way in range(2):
            found[1, way][0].wait_recv()
            piece = region(1, way)
            total[piece] += r[way, 1, piece].astype(F32)
        out[...] = total[...].astype(BF16)
        sent = []
        for o in range(1, b):
            mate = lax.rem(mine_j + o, b)
            c = to_mp(
                out.at[mate], sw.at[o], sw_ss.at[which, o], sw_rs.at[which, o],
                mine_i * b + mate,
            )
            c.start()
            sent.append(c)
        return sent

    sent_q = finish(0, hops_q, tq, rq, sq, oq, swq)
    relay(hops_kv, tkv, rkv)
    sent_kv = finish(1, hops_kv, tkv, rkv, skv, okv, swkv)

    def columns(j, k):
        return pl.ds(pl.multiple_of(k * width + j * wide, LANES), wide)

    dwq[:, columns(mine_j, 0)] = oq[mine_j]
    for o in range(1, b):
        source = lax.rem(mine_j + b - o, b)
        sent_q[o - 1].wait_recv()
        dwq[:, columns(source, 0)] = swq[o]
    for k in range(2):
        dwkv[:, columns(mine_j, k)] = okv[mine_j][:, k * wide : (k + 1) * wide]
    for o in range(1, b):
        source = lax.rem(mine_j + b - o, b)
        sent_kv[o - 1].wait_recv()
        for k in range(2):
            dwkv[:, columns(source, k)] = swkv[o][:, k * wide : (k + 1) * wide]

    for c in feat + crossing + half + ret_copies + sent_q + sent_kv:
        c.wait_send()
    for c, _ in list(hops_q.values()) + list(hops_kv.values()):
        c.wait_send()
    for o in range(1, n):
        got(dq_s.at[0], dq_all.at[me], dq_ss.at[o], dq_rs.at[o]).wait_send()
        got(dkv_s.at[0], dkv_all.at[me], dkv_ss.at[o], dkv_rs.at[o]).wait_send()


def write_out(d_grid, d_nodes, dw_query, dw_keyval, out_grid, out_nodes, out_q, out_kv):
    out_grid[...] = d_grid[...]
    out_nodes[...] = d_nodes[...]
    out_q[...] = dw_query[...].astype(F32)
    out_kv[...] = dw_keyval[...].astype(F32)


def per_device(grid_feat, node_feat, cotangent, w_query, w_keyval, neighbours, send_rows):
    n = lax.axis_size("mp")
    nd = lax.axis_size("dp")
    samples_dev, grid_dev, width = grid_feat.shape
    nodes = node_feat.shape[1]
    cap = send_rows.shape[2]
    slots = n * cap
    rows = slots + nodes
    a = 2
    b = n // a
    high = width // a
    wide = width // b
    out_rows = width // (n * nd)
    per = LANES * HEADS // width
    wscale = 1.0 / math.sqrt(samples_dev * nd * grid_dev * n)
    vmem = pl.BlockSpec(memory_space=pltpu.VMEM)
    anywhere = pl.BlockSpec(memory_space=pl.ANY)
    dma = pltpu.SemaphoreType.DMA
    d_grid, d_nodes, dw_query, dw_keyval = pl.pallas_call(
        functools.partial(kernel, n, nd, wscale),
        out_shape=(
            jax.ShapeDtypeStruct((grid_dev, width), BF16),
            jax.ShapeDtypeStruct((nodes, width), BF16),
            jax.ShapeDtypeStruct((out_rows, width), BF16),
            jax.ShapeDtypeStruct((out_rows, 2 * width), BF16),
        ),
        in_specs=[vmem, vmem, vmem, anywhere, anywhere, vmem, vmem],
        out_specs=(vmem, vmem, vmem, vmem),
        scratch_shapes=[
            pltpu.VMEM((width, width), BF16),
            pltpu.VMEM((width, 2 * width), BF16),
            pltpu.VMEM((slots, width), BF16),
            pltpu.VMEM((rows, width), BF16),
            pltpu.VMEM((grid_dev, width), BF16),
            pltpu.VMEM((rows, 2 * width), BF16),
            pltpu.VMEM((per * grid_dev, rows), F32),
            pltpu.VMEM((n, grid_dev, high), BF16),
            pltpu.VMEM((n, nodes, high), BF16),
            pltpu.VMEM((b, grid_dev, wide), BF16),
            pltpu.VMEM((n, grid_dev, wide), BF16),
            pltpu.VMEM((b, rows, 2 * wide), BF16),
            pltpu.VMEM((b, slots, 2 * wide), BF16),
            pltpu.VMEM((b, nodes, 2 * wide), BF16),
            pltpu.VMEM((n, nodes, 2 * wide), BF16),
            pltpu.VMEM((nd, b, out_rows, wide), BF16),
            pltpu.VMEM((nd, b, out_rows, 2 * wide), BF16),
            pltpu.VMEM((2, nd // 2 + 1, b, out_rows, wide), BF16),
            pltpu.VMEM((2, nd // 2 + 1, b, out_rows, 2 * wide), BF16),
            pltpu.VMEM((b, out_rows, wide), F32),
            pltpu.VMEM((b, out_rows, 2 * wide), F32),
            pltpu.VMEM((b, out_rows, wide), BF16),
            pltpu.VMEM((b, out_rows, 2 * wide), BF16),
            pltpu.VMEM((b, out_rows, wide), BF16),
            pltpu.VMEM((b, out_rows, 2 * wide), BF16),
            pltpu.VMEM((nodes, slots), F32),
            dma((2,)),
            dma((n,)), dma((n,)),
            dma((2, 2 * b)), dma((2, 2 * b)),
            dma((n,)), dma((n,)),
            dma((b, n)), dma((b, n)),
            dma((n,)), dma((n,)),
            dma((2, 2, nd // 2 + 1)), dma((2, 2, nd // 2 + 1)),
            dma((2, b)), dma((2, b)),
        ],
        compiler_params=pltpu.CompilerParams(
            collective_id=0, has_side_effects=True, vmem_limit_bytes=56 * 1024 * 1024
        ),
        name="graph_attention_grads",
    )(
        grid_feat[0], node_feat[0], cotangent[0], w_query, w_keyval, neighbours.T, send_rows[0],
    )
    d_grid, d_nodes, dw_query, dw_keyval = pl.pallas_call(
        write_out,
        out_shape=(
            jax.ShapeDtypeStruct((grid_dev, width), BF16),
            jax.ShapeDtypeStruct((nodes, width), BF16),
            jax.ShapeDtypeStruct((out_rows, width), F32),
            jax.ShapeDtypeStruct((out_rows, 2 * width), F32),
        ),
        in_specs=[vmem, vmem, vmem, vmem],
        out_specs=(vmem, vmem, vmem, vmem),
        name="write_out",
    )(d_grid, d_nodes, dw_query, dw_keyval)
    return d_grid[None], d_nodes[None], dw_query, dw_keyval


def solution(mesh):
    in_specs = (
        P(("groups", "dp"), "mp", None),
        P(("groups", "dp"), "mp", None),
        P(("groups", "dp"), "mp", None),
        P(),
        P(),
        P("mp", None),
        P("mp", None, None),
    )
    out_specs = (
        P(("groups", "dp"), "mp", None),
        P(("groups", "dp"), "mp", None),
        P(("groups", "mp", "dp"), None),
        P(("groups", "mp", "dp"), None),
    )
    return jax.shard_map(
        per_device, mesh=mesh, in_specs=in_specs, out_specs=out_specs, check_vma=False
    )
```
